512 devices in a mesh: dp: 32 (over x, z), ctx: 16 (over y, core).
Axes of the slice: x: 4, y: 8, z: 8, core: 2. Of those that a mesh axis runs over, the one named last changes fastest.
Arguments:
- u_codes: bfloat16 [32, 4096, 2560], P('dp', 'ctx'), may hold values from -384 to 384
- u_scale: float32 [32, 4096, 20], P('dp', 'ctx'), may hold values from 0.0078125 to 0.03125
- w_bc: bfloat16 [2560, 256], P('ctx'), may hold values from -0.125 to 0.125
- xs: bfloat16 [32, 4096, 2560], P('dp', 'ctx'), may hold values from -6 to 6
- dt: float32 [32, 40, 4096], P('dp', None, 'ctx'), may hold values from 0.0078125 to 0.03125
- log_keep: float32 [32, 40, 4096], P('dp', None, 'ctx'), may hold values from -1.2 to 0, as said below
- dy: bfloat16 [32, 4096, 2560], P('dp', 'ctx'), may hold values from -0.0010299683 to 0.0010299683
- lengths: int32 [32, 2], P('dp'), may hold values from 0 to 4096, as said below
Outputs:
- grad_bc: float32 [2560, 256], P(('dp', 'ctx'))
- grad_dt: float32 [32, 40, 4096], P('dp', None, 'ctx')
- grad_keep: float32 [32, 40, 4096], P('dp', None, 'ctx')
The draws below stay inside these ranges and needn't reach their ends.
Inputs may be any that keep to these rules, and one draw needn't show every extreme that they name: `lengths`: each row sums to 4096; some rows start with 0 (no document boundary inside the sequence), row 0 among them. `log_keep`: non-positive.
All inputs are finite; a program needn't handle non-finite values.
Results may differ from the reference program's by a relative error of at most 0.006.
Values may be sent and summed in bfloat16 or wider, within the bound.
A program may use at most 128 MiB of HBM per device.

```python
import math
import jax
import jax.numpy as jnp
from jax import lax

D = 2560
H = 40
P_SIZE = 64
N = 128
CH = 256
QB = 128
TOK_DEV = 256
SEQ = 4096
BATCH = 32
HP = 2560


def draw_lengths(key, part):
    split = jax.random.randint(key, (BATCH,), 0, SEQ)
    split = jnp.where(jnp.arange(BATCH) == 0, 0, split)
    return jnp.stack([split, SEQ - split], axis=1).astype(jnp.int32)


def draw_log_keep(key, part):
    keys = jax.random.split(key, 7)
    fast_share = 0.5
    fast = jax.random.bernoulli(keys[0], fast_share, (BATCH, H))
    fast_rate = jnp.exp(jax.random.uniform(keys[1], (BATCH, H), jnp.float32, math.log(1.0 / 60.0), math.log(1.0 / 30.0)))
    slow_rate = jnp.exp(jax.random.uniform(keys[2], (BATCH, H), jnp.float32, math.log(0.1), math.log(0.6))) / SEQ
    reset_rate = jnp.where(fast, fast_rate, slow_rate)
    device_blocks = SEQ // TOK_DEV
    block_scale_factor = jnp.exp(jax.random.uniform(keys[3], (BATCH, H, device_blocks), jnp.float32, math.log(0.5), math.log(2.0)))
    block_scale_factor = jnp.repeat(block_scale_factor, TOK_DEV, axis=2)
    token_scale_factor = jnp.exp(jax.random.uniform(keys[4], (BATCH, H, SEQ), jnp.float32, math.log(0.5), math.log(2.0)))
    reset_locations = jax.random.randint(keys[5], (BATCH, 2), 0, SEQ)
    step_amounts = jax.random.uniform(keys[6], (BATCH, 2), jnp.float32, 0.22, 0.5)
    reset_position = jnp.arange(SEQ)
    reset_cluster = jnp.sum((reset_position[None, None, :] == reset_locations[:, :, None]).astype(jnp.float32) * step_amounts[:, :, None], axis=1)
    return -(reset_rate[:, :, None] * block_scale_factor * token_scale_factor) - reset_cluster[:, None, :]


def raised(drawn, key, source, target, blocks, factor):
    def block_of(axis_at):
        return (jnp.arange(drawn.shape[axis_at]) // (drawn.shape[axis_at] // blocks)).reshape((-1,) + (1,) * (drawn.ndim - 1 - axis_at))

    near = jax.random.permutation(key, blocks)[block_of(target)]
    far = (block_of(target) + blocks // 2) % blocks
    return jnp.where((block_of(source) == near) | (block_of(source) == far), factor * drawn, drawn)


def steps_of(own_key, dims, cuts, low, largest):
    loudness, own = 1.0, jax.random.fold_in(own_key, 6)
    for dim, shards_of in cuts:
        heights = jnp.exp(jax.random.uniform(jax.random.fold_in(own, dim), (shards_of,), jnp.float32, low / len(cuts), largest / len(cuts)))
        loudness = loudness * jnp.repeat(heights, dims[dim] // shards_of).reshape([-1 if axis == dim else 1 for axis in range(len(dims))])
    return loudness


def noise(rng, dims, width, limit, pieces=(), kind=jnp.bfloat16):
    result = jax.random.normal(rng, dims, jnp.float32) * width
    if len(pieces) > 0:
        result = steps_of(rng, dims, pieces, -0.22, 0.18) * result
    return jnp.clip(result, min=-limit, max=limit).astype(kind)


def gaussian_with(stream_key, dims, width, reach, cuts, heavy, held_as=jnp.bfloat16):
    array = width * jax.random.normal(stream_key, dims, jnp.float32)
    if cuts:
        array = array * steps_of(stream_key, dims, cuts, -0.22, 0.18)
    return jnp.clip(raised(array, jax.random.fold_in(stream_key, 3), *heavy), -reach, reach).astype(held_as)


def setup_inputs(seed: int = 0) -> dict:
    key_of = jax.random.split(jax.random.key(seed), 9)
    return {
        "u_codes": gaussian_with(key_of[0], (BATCH, SEQ, D), 64.0, 384.0, ((0, 32), (1, 16)), (1, 2, 16, 2.0)),
        "u_scale": jnp.clip(jnp.exp(math.log(0.03125) - 1.3862944 * jax.random.uniform(key_of[1], (BATCH, SEQ, D // QB), jnp.float32) ** steps_of(key_of[1], (BATCH, SEQ, D // QB), ((0, 32), (1, 16)), -0.2, 0.2)), 0.0078125, 0.03125),
        "w_bc": noise(key_of[2], (D, 2 * N), D ** -0.5, 0.125, ((0, 16),)),
        "xs": noise(key_of[3], (BATCH, SEQ, HP), 1.0, 6.0, ((0, 32), (1, 16))),
        "dt": jnp.clip(jnp.exp(math.log(0.03125) - 1.3862944 * jax.random.uniform(key_of[4], (BATCH, H, SEQ), jnp.float32) ** steps_of(key_of[4], (BATCH, H, SEQ), ((0, 32), (2, 16)), -0.2, 0.2)), 0.0078125, 0.03125),
        "log_keep": draw_log_keep(jax.random.fold_in(key_of[8], 71), 0),
        "dy": noise(key_of[6], (BATCH, SEQ, HP), ((SEQ * P_SIZE * N) ** -0.5), 0.0010299683, ((0, 32), (1, 16))),
        "lengths": draw_lengths(jax.random.fold_in(key_of[8], 71), 0),
    }


highest = lax.Precision.HIGHEST


def block_setup(keep, resets):
    cumlog = jnp.cumsum(keep, axis=1)
    counts = jnp.cumsum(resets)
    final_log = cumlog[:, -1:]
    final_count = counts[-1]
    dec_start = jnp.exp(cumlog) * (counts == 0).astype(jnp.float32)[None, :]
    dec_end = jnp.exp(final_log - cumlog) * (counts == final_count).astype(jnp.float32)[None, :]
    carry = jnp.exp(final_log[:, 0]) * (final_count == 0).astype(jnp.float32)
    return cumlog, counts, dec_start, dec_end, carry


def intra_terms(x_rows, dy_rows, steps, cumlog, batch_c, batch_b, same, lower, cross):
    diff = cumlog[:, :, None] - cumlog[:, None, :]
    weight = jnp.where(same[None], jnp.exp(jnp.minimum(diff, 0.0)), 0.0)
    dots = jnp.einsum("thp,shp->hts", dy_rows.astype(jnp.float32), x_rows.astype(jnp.float32))
    mixed = weight * dots
    scaled = (mixed * steps[:, None, :]).astype(jnp.bfloat16)
    grad_c = jnp.einsum("hts,sn->tn", scaled.astype(jnp.float32), batch_b.astype(jnp.float32))
    grad_b = jnp.einsum("hts,tn->sn", scaled.astype(jnp.float32), batch_c.astype(jnp.float32))
    paired = mixed * cross[None]
    grad_step = jnp.sum(paired, axis=1)
    weighted = paired * steps[:, None, :]
    before = jnp.cumsum(weighted, axis=2) - weighted
    grad_log = jnp.sum(jnp.where(lower[None], before, 0.0), axis=1)
    return grad_c, grad_b, grad_step, grad_log


def finish(x_full, dy_full, b_full, c_full, steps, dec_start, dec_end, carry, s_in, g_after):
    y_inter = jnp.einsum("hpn,tn->htp", s_in, c_full, precision=highest) * dec_start[:, :, None]
    x_term = jnp.einsum("thp,htp->ht", dy_full, y_inter, precision=highest)
    grad_c = jnp.einsum("ht,thp,hpn->tn", dec_start, dy_full, s_in, precision=highest)
    g_on_b = jnp.einsum("hpn,tn->htp", g_after, b_full, precision=highest)
    external = dec_end * jnp.einsum("thp,htp->ht", x_full, g_on_b, precision=highest)
    grad_b = jnp.einsum("ht,thp,hpn->tn", dec_end * steps, x_full, g_after, precision=highest)
    constant = carry * jnp.sum(g_after * s_in, axis=(1, 2))
    later = jnp.cumsum(x_term[:, ::-1], axis=1)[:, ::-1]
    z_term = steps * external
    earlier = jnp.cumsum(z_term, axis=1) - z_term
    return grad_c, grad_b, external, later + earlier + constant[:, None]


def one_sequence(item, w_bc):
    codes, scales, xs, steps, keep, cotan, lengths = item
    u_deq = (codes.astype(jnp.float32).reshape(SEQ, D // QB, QB) * scales[:, :, None]).reshape(SEQ, D).astype(jnp.bfloat16)
    proj = jnp.dot(u_deq, w_bc, preferred_element_type=jnp.float32).astype(jnp.bfloat16)
    position = jnp.arange(SEQ, dtype=jnp.int32)
    starts = (jnp.cumsum(lengths) - lengths).astype(jnp.int32)
    resets = jnp.any(position[:, None] == starts[None, :], axis=1).astype(jnp.float32)
    nblock = SEQ // CH
    lower = jnp.arange(CH)[:, None] >= jnp.arange(CH)[None, :]
    items = (xs.reshape(nblock, CH, H, P_SIZE), cotan.reshape(nblock, CH, H, P_SIZE),
             proj[:, :N].reshape(nblock, CH, N), proj[:, N:].reshape(nblock, CH, N),
             steps.reshape(H, nblock, CH).transpose(1, 0, 2), keep.reshape(H, nblock, CH).transpose(1, 0, 2),
             resets.reshape(nblock, CH))

    def local(block):
        x_rows, dy_rows, batch_b, batch_c, step_rows, keep_rows, reset_rows = block
        cumlog, counts, dec_start, dec_end, carry = block_setup(keep_rows, reset_rows)
        same = lower & (counts[:, None] == counts[None, :])
        cross = jnp.dot(batch_c, batch_b.T, preferred_element_type=jnp.float32)
        x_full = x_rows.astype(jnp.float32)
        dy_full = dy_rows.astype(jnp.float32)
        b_full = batch_b.astype(jnp.float32)
        c_full = batch_c.astype(jnp.float32)
        s_local = jnp.einsum("ht,thp,tn->hpn", dec_end * step_rows, x_full, b_full, precision=highest)
        g_local = jnp.einsum("ht,thp,tn->hpn", dec_start, dy_full, c_full, precision=highest)
        inner = intra_terms(x_rows, dy_rows, step_rows, cumlog, batch_c, batch_b, same, lower, cross)
        return carry, s_local, g_local, dec_start, dec_end, inner

    carries, s_locals, g_locals, dec_starts, dec_ends, inner = lax.map(local, items)

    def forward(state, elem):
        return elem[0][:, None, None] * state + elem[1], state

    zeros = jnp.zeros((H, P_SIZE, N), jnp.float32)
    _, s_ins = lax.scan(forward, zeros, (carries, s_locals))
    _, g_afters = lax.scan(forward, zeros, (carries, g_locals), reverse=True)

    def final(block):
        x_rows, dy_rows, batch_b, batch_c, step_rows, dec_start, dec_end, carry, s_in, g_after = block
        return finish(x_rows.astype(jnp.float32), dy_rows.astype(jnp.float32), batch_b.astype(jnp.float32),
                      batch_c.astype(jnp.float32), step_rows, dec_start, dec_end, carry, s_in, g_after)

    outer_c, outer_b, external, outer_log = lax.map(final, (items[0], items[1], items[2], items[3], items[4],
                                                           dec_starts, dec_ends, carries, s_ins, g_afters))
    grad_c = inner[0] + outer_c
    grad_b = inner[1] + outer_b
    dbc = jnp.concatenate([grad_b, grad_c], axis=2).reshape(SEQ, 2 * N).astype(jnp.bfloat16)
    grad_w = jnp.dot(u_deq.T, dbc, preferred_element_type=jnp.float32)
    grad_step = (inner[2] + external).transpose(1, 0, 2).reshape(H, SEQ)
    grad_log = (inner[3] + outer_log).transpose(1, 0, 2).reshape(H, SEQ)
    return grad_w, grad_step, grad_log


def reference(u_codes, u_scale, w_bc, xs, dt, log_keep, dy, lengths):
    def per_sequence(total, item):
        grad_w, grad_step, grad_log = one_sequence(item, w_bc)
        return total + grad_w, (grad_step, grad_log)

    total, (grad_dt, grad_keep) = lax.scan(per_sequence, jnp.zeros((D, 2 * N), jnp.float32),
                                           (u_codes, u_scale, xs, dt, log_keep, dy, lengths))
    return total, grad_dt, grad_keep
```

```python
import functools

import jax
import jax.numpy as jnp
from jax import lax
from jax.experimental import pallas as pl
from jax.experimental.pallas import tpu as pltpu
from jax.sharding import PartitionSpec as P

D = 2560
H = 40
P_SIZE = 64
N = 128
CH = 256
QB = 128
HALF = H * P_SIZE // 2
NY = 8
NX = 4
NZ = 8
ROWS_W = 160
CHUNK = 128
NCHUNK = HALF // CHUNK
SKEW = 3
SLOTS = max(NCHUNK + SKEW * (NY - 1), H // 2)
BLK = 512
F32 = jnp.float32
BF16 = jnp.bfloat16
MESH = pl.DeviceIdType.MESH
EXACT = lax.Precision.HIGHEST
NT = (((1,), (1,)), ((), ()))
TN = (((0,), (0,)), ((), ()))


def dot(a, b, dims=None, precision=None):
    if dims is None:
        dims = (((1,), (0,)), ((), ()))
    return lax.dot_general(a, b, dims, precision=precision, preferred_element_type=F32)


def split(v):
    hi = v.astype(BF16)
    return hi, (v - hi.astype(F32)).astype(BF16)


def dot2(pair, b, dims=None):
    return dot(pair[0], b, dims) + dot(pair[1], b, dims)


def where_am_i():
    dp = lax.axis_index("dp")
    ctx = lax.axis_index("ctx")
    return dp, ctx, lax.div(ctx, 2), lax.rem(ctx, 2)


def rcopy(src, dst, send, recv, dev):
    return pltpu.make_async_remote_copy(
        src_ref=src, dst_ref=dst, send_sem=send, recv_sem=recv, device_id=dev, device_id_type=MESH
    )


def greet(peers):
    barrier = pltpu.get_barrier_semaphore()
    for dev in peers:
        pl.semaphore_signal(barrier, inc=1, device_id=dev, device_id_type=MESH)
    return barrier, len(peers)


def project_kernel(codes_ref, scale_ref, w_ref, u_ref, proj_ref, w_all, s1, r1, s2, r2, lsem):
    dp, ctx, y, c = where_am_i()
    partner = (dp, 2 * y + 1 - c)
    ydev = [(dp, lax.rem(y + d, NY) * 2 + c) for d in range(NY)]
    barrier, count = greet([partner] + ydev[1:])
    pl.semaphore_wait(barrier, count)

    def rows(i):
        return pl.ds(pl.multiple_of(i * ROWS_W, 32), ROWS_W)

    order = (4, 3, 5, 2, 6, 1, 7)
    sends = {}
    for d in order:
        sends[d] = rcopy(w_ref, w_all.at[rows(ctx)], s1.at[d], r1.at[d], ydev[d])
        sends[d].start()
    relay = {0: rcopy(w_ref, w_all.at[rows(ctx)], s2.at[0], r2.at[0], partner)}
    relay[0].start()
    local = pltpu.make_async_copy(w_ref, w_all.at[rows(ctx)], lsem)
    local.start()
    for j in range(D // QB):
        at = slice(j * QB, (j + 1) * QB)
        u_ref[:, at] = (codes_ref[:, at].astype(F32) * scale_ref[:, j : j + 1]).astype(BF16)
    local.wait()
    for d in (1, 7, 2, 6, 3, 5, 4):
        sends[d].wait_recv()
        got = rows(lax.rem(y + NY - d, NY) * 2 + c)
        relay[d] = rcopy(w_all.at[got], w_all.at[got], s2.at[d], r2.at[d], partner)
        relay[d].start()
    for d in range(NY):
        relay[d].wait_recv()
    proj_ref[...] = dot(u_ref[...], w_all[...]).astype(BF16)
    for d in order:
        sends[d].wait_send()
    for d in range(NY):
        relay[d].wait_send()


def mixer_kernel(
    marks, x_ref, dy_ref, proj_ref, dt_ref, keep_ref, gdt_ref, gkeep_ref, dbc_ref,
    dyw, xw, sloc, gloc, prt_s, prt_g, c_own, c_prt,
    fsend, frecv, vsend, vrecv, s_all, g_all, os, og,
    racc, cacc, ssum, bound, cross, cumr, cum_t, ds_t, de_t, dt_t,
    ps, pr, fs, fr, vs, vr, oss, osr, ogs, ogr,
):
    dp, ctx, y, c = where_am_i()
    partner = (dp, 2 * y + 1 - c)
    ahead = (dp, lax.rem(y + 1, NY) * 2 + c)
    behind = (dp, lax.rem(y + NY - 1, NY) * 2 + c)
    barrier, count = greet([partner, ahead, behind])
    r_eff, r_end, limit = marks[0], marks[1], marks[2]

    def iota(shape, dim):
        return lax.broadcasted_iota(jnp.int32, shape, dim)

    row, col = iota((CH, CH), 0), iota((CH, CH), 1)
    same = jnp.where(row >= r_eff, 1, 0) == jnp.where(col >= r_eff, 1, 0)
    bound[...] = jnp.where((col <= row) & same, 0.0, -1e30)
    upto = jnp.where(row <= col, 1.0, 0.0)
    eye = jnp.where(row == col, 1.0, 0.0)
    pad = jnp.zeros((128 - H, CH), F32)
    keep_p = jnp.concatenate([keep_ref[...], pad], axis=0)
    cum_p = dot(keep_p, upto, precision=EXACT)
    cumr[...] = cum_p[:H]
    cum = jnp.transpose(cum_p)
    cum_t[...] = cum
    dts = jnp.transpose(jnp.concatenate([dt_ref[...], pad], axis=0))
    tcol = iota((CH, 128), 0)
    ds = jnp.where(tcol < limit, jnp.exp(cum), 0.0)
    de = jnp.where(tcol >= r_end, jnp.exp(cum[CH - 1 : CH, :] - cum), 0.0)
    ds_t[...] = ds
    de_t[...] = de
    dt_t[...] = dts
    carry = jnp.where(CH - 1 < limit, jnp.exp(cum_p[:H, CH - 1 : CH]), 0.0)
    c_own[...] = jnp.broadcast_to(carry, (H, 128))

    def halves(v):
        return jnp.concatenate(split(v), axis=1)

    ds_hl, ws_hl = halves(ds), halves(de * dts)
    b_mat, c_mat = proj_ref[:, :N], proj_ref[:, N:]

    def local_states(g, _):
        at = pl.ds(pl.multiple_of(g * BLK, BLK), BLK)
        head = lax.rem(iota((CH, BLK), 0), 128)
        spread = jnp.where(head == 8 * g + lax.div(iota((CH, BLK), 1), P_SIZE), 1.0, 0.0).astype(BF16)
        dyb = split(dy_ref[:, at].astype(F32) * dot(ds_hl, spread))
        xb = split(x_ref[:, at].astype(F32) * dot(ws_hl, spread))
        for n in range(2):
            dyw[n, :, at] = dyb[n]
            xw[n, :, at] = xb[n]
        sloc[at, :] = dot2(xb, b_mat, TN)
        gloc[at, :] = dot2(dyb, c_mat, TN)
        return 0

    lax.fori_loop(0, H * P_SIZE // BLK, local_states, 0)
    pl.semaphore_wait(barrier, count)
    mine = pl.multiple_of(c * HALF, 128)
    theirs = pl.ds(pl.multiple_of((1 - c) * HALF, 128), HALF)
    swap = [
        rcopy(c_own, c_prt, ps.at[0], pr.at[0], partner),
        rcopy(sloc.at[theirs], prt_s, ps.at[1], pr.at[1], partner),
        rcopy(gloc.at[theirs], prt_g, ps.at[2], pr.at[2], partner),
    ]
    for one in swap:
        one.start()

    cross[...] = dot(c_mat, b_mat, NT)
    ssum[...] = jnp.zeros_like(ssum)
    racc[...] = jnp.zeros_like(racc)

    @pl.when(y == 0)
    def _():
        frecv[...] = jnp.zeros_like(frecv)

    @pl.when(y == NY - 1)
    def _():
        vrecv[...] = jnp.zeros_like(vrecv)

    lane = iota((CH, 128), 1)
    first = c == 0

    def chunk_rows(i):
        return pl.ds(pl.multiple_of(i * CHUNK, CHUNK), CHUNK)

    def decay(ref, i):
        h = c * (H // 2) + 2 * i
        return jnp.concatenate(
            [jnp.broadcast_to(ref[pl.ds(h + j, 1), :], (P_SIZE, N)) for j in range(2)], axis=0
        )

    def pick(i, own, other):
        a = own[pl.ds(pl.multiple_of(mine + i * CHUNK, CHUNK), CHUNK), :]
        b = other[chunk_rows(i), :]
        return jnp.where(first, a, b), jnp.where(first, b, a)

    def f_copy(i):
        return rcopy(fsend.at[chunk_rows(i)], frecv.at[chunk_rows(i)], fs.at[i], fr.at[i], ahead)

    def v_copy(i):
        return rcopy(vsend.at[chunk_rows(i)], vrecv.at[chunk_rows(i)], vs.at[i], vr.at[i], behind)

    def full_rows(i):
        return pl.ds(pl.multiple_of(mine + i * CHUNK, CHUNK), CHUNK)

    def s_copy(i):
        return rcopy(os.at[chunk_rows(i)], s_all.at[full_rows(i)], oss.at[i], osr.at[i], partner)

    def g_copy(i):
        return rcopy(og.at[chunk_rows(i)], g_all.at[full_rows(i)], ogs.at[i], ogr.at[i], partner)

    def slot(k, _):
        @pl.when(k < H // 2)
        def _():
            at = pl.ds(pl.multiple_of(k * 128, 128), 128)
            x2, dy2 = x_ref[:, at], dy_ref[:, at]
            turned = pltpu.roll(cum_t[...], lax.rem(128 - 2 * k, 128), 1)
            for j in range(2):
                h = 2 * k + j
                xm = jnp.where((lane < P_SIZE) if j == 0 else (lane >= P_SIZE), x2, jnp.zeros_like(x2))
                dots = dot(dy2, xm, NT)
                diff = turned[:, j : j + 1] - cumr[pl.ds(h, 1), :]
                mixed = jnp.exp(jnp.minimum(diff, bound[...])) * dots
                pair = mixed * cross[...]
                steps = dt_ref[pl.ds(h, 1), :]
                ssum[...] += mixed * steps
                cacc[pl.ds(h, 1), :] = jnp.sum(pair, axis=0, keepdims=True)
                rsum = jnp.sum(pair * steps, axis=1, keepdims=True)
                racc[...] += jnp.where(lane == h, rsum, 0.0)

        @pl.when(k == 0)
        def _():
            for one in swap:
                one.wait_recv()

        i = k - SKEW * y

        @pl.when((i >= 0) & (i < NCHUNK))
        def _():
            @pl.when(y > 0)
            def _():
                f_copy(i).wait_recv()

            a0, a1 = decay(c_own, i), decay(c_prt, i)
            a0, a1 = jnp.where(first, a0, a1), jnp.where(first, a1, a0)
            s0, s1 = pick(i, sloc, prt_s)
            state = frecv[chunk_rows(i), :].astype(F32)
            mid = a0 * state + s0

            @pl.when(y < NY - 1)
            def _():
                fsend[chunk_rows(i), :] = (a1 * mid + s1).astype(BF16)
                f_copy(i).start()

            os[chunk_rows(i), :] = jnp.where(first, mid, state)
            s_copy(i).start()
            s_all[full_rows(i), :] = jnp.where(first, state, mid)

        q = k - SKEW * (NY - 1 - y)

        @pl.when((q >= 0) & (q < NCHUNK))
        def _():
            @pl.when(y < NY - 1)
            def _():
                v_copy(q).wait_recv()

            a0, a1 = decay(c_own, q), decay(c_prt, q)
            a0, a1 = jnp.where(first, a0, a1), jnp.where(first, a1, a0)
            g0, g1 = pick(q, gloc, prt_g)
            state = vrecv[chunk_rows(q), :].astype(F32)
            mid = a1 * state + g1

            @pl.when(y > 0)
            def _():
                vsend[chunk_rows(q), :] = (a0 * mid + g0).astype(BF16)
                v_copy(q).start()

            og[chunk_rows(q), :] = jnp.where(first, state, mid)
            g_copy(q).start()
            g_all[full_rows(q), :] = jnp.where(first, mid, state)

        return 0

    lax.fori_loop(0, SLOTS, slot, 0)

    def drain(i, _):
        s_copy(i).wait()
        g_copy(i).wait()

        @pl.when(y < NY - 1)
        def _():
            f_copy(i).wait_send()

        @pl.when(y > 0)
        def _():
            v_copy(i).wait_send()

        return 0

    lax.fori_loop(0, NCHUNK, drain, 0)
    for one in swap:
        one.wait_send()

    def outer(g, sums):
        x_t, e_t, gc, gb_, const = sums
        at = pl.ds(pl.multiple_of(g * BLK, BLK), BLK)
        s_blk, g_blk = s_all[at, :], g_all[at, :]
        gather = jnp.where(8 * g + lax.div(iota((BLK, 128), 0), P_SIZE) == iota((BLK, 128), 1), 1.0, 0.0).astype(BF16)
        fold = jnp.where(8 * g + lax.div(iota((128, BLK), 1), P_SIZE) == iota((128, BLK), 0), 1.0, 0.0).astype(BF16)
        both = split(s_blk * g_blk)
        s_blk, g_blk = split(s_blk), split(g_blk)
        inner_y = dot(c_mat, s_blk[0], NT) + dot(c_mat, s_blk[1], NT)
        inner_x = dot(b_mat, g_blk[0], NT) + dot(b_mat, g_blk[1], NT)
        prod_y = split(dy_ref[:, at].astype(F32) * inner_y)
        prod_x = split(x_ref[:, at].astype(F32) * inner_x)
        return (
            x_t + dot2(prod_y, gather),
            e_t + dot2(prod_x, gather),
            gc + dot2((dyw[0, :, at], dyw[1, :, at]), s_blk[0]) + dot(dyw[0, :, at], s_blk[1]),
            gb_ + dot2((xw[0, :, at], xw[1, :, at]), g_blk[0]) + dot(xw[0, :, at], g_blk[1]),
            const + dot(fold, both[0]) + dot(fold, both[1]),
        )

    sums = split(ssum[...])
    zero = jnp.zeros((CH, 128), F32)
    start = (zero, zero, dot2(sums, b_mat), dot2(sums, c_mat, TN), jnp.zeros((128, 128), F32))
    x_t, e_t, gc, gb_, const = lax.fori_loop(0, H * P_SIZE // BLK, outer, start)
    dbc_ref[:, :N] = gb_.astype(BF16)
    dbc_ref[:, N:] = gc.astype(BF16)
    ext_t = e_t * de_t[...]
    ext = jnp.transpose(ext_t)[:H]
    z = jnp.transpose(ext_t * dt_t[...])[:H]
    late = jnp.transpose(x_t * ds_t[...] + racc[...])[:H]
    gdt_ref[...] = cacc[...] + ext
    since = jnp.where(row >= col, 1.0, 0.0)
    before = jnp.where(row < col, 1.0, 0.0)
    total = jnp.sum(const, axis=1, keepdims=True)[:H] * c_own[:, :1]
    gkeep_ref[...] = (
        dot(late - cacc[...] * dt_ref[...], since, precision=EXACT) + dot(z, before, precision=EXACT) + total
    )


def reduce_kernel(
    u_ref, dbc_ref, out_ref, own, psend, precv, xsend, xrecv, zsum, zsend, zrecv, tsend, trecv,
    ps, pr, xs_, xr, zs, zr, ts, tr,
):
    dp, ctx, y, c = where_am_i()
    x, z = lax.div(dp, NZ), lax.rem(dp, NZ)
    partner = (dp, 2 * y + 1 - c)
    xdev = [(lax.rem(x + d, NX) * NZ + z, ctx) for d in range(NX)]
    zdev = [(x * NZ + lax.rem(z + d, NZ), ctx) for d in range(NZ)]
    tdev = [(dp, lax.rem(ctx + d, 2 * NY)) for d in range(2 * NY)]
    barrier, count = greet(xdev[1:] + zdev[1:] + tdev[1:])
    first = c == 0
    d_b, d_c = dbc_ref[:, :N], dbc_ref[:, N:]
    d_own = jnp.where(first, d_b, d_c)
    d_oth = jnp.where(first, d_c, d_b)
    span = D // NX
    piece = span // NZ
    order = (2, 1, 3, 0)

    def cols(d):
        return pl.ds(pl.multiple_of(lax.rem(x + d, NX) * span, 128), span)

    pc = {}
    for n, d in enumerate(order):
        psend[d] = dot(u_ref[:, cols(d)], d_oth, TN)
        if n == 0:
            pl.semaphore_wait(barrier, count)
        pc[d] = rcopy(psend.at[d], precv.at[d], ps.at[d], pr.at[d], partner)
        pc[d].start()
    xc = {}
    for d in order:
        part = dot(u_ref[:, cols(d)], d_own, TN)
        pc[d].wait_recv()
        if d == 0:
            own[...] = part + precv[0]
        else:
            xsend[d] = (part + precv[d]).astype(BF16)
            xc[d] = rcopy(xsend.at[d], xrecv.at[d], xs_.at[d], xr.at[d], xdev[d])
            xc[d].start()
    for d in (1, 3, 2):
        xc[d].wait_recv()
    zsum[...] = own[...] + xrecv[1].astype(F32) + xrecv[2].astype(F32) + xrecv[3].astype(F32)
    zc = {}
    for d in (4, 3, 5, 2, 6, 1, 7):
        at = pl.ds(pl.multiple_of(lax.rem(z + d, NZ) * piece, 16), piece)
        zsend[d] = zsum[at, :].astype(BF16)
        zc[d] = rcopy(zsend.at[d], zrecv.at[d], zs.at[d], zr.at[d], zdev[d])
        zc[d].start()
    total = zsum[pl.ds(pl.multiple_of(z * piece, 16), piece), :]
    for d in (1, 7, 2, 6, 3, 5, 4):
        zc[d].wait_recv()
        total = total + zrecv[d].astype(F32)
    tsend[...] = jnp.zeros_like(tsend)
    for i in range(2 * NY):
        tsend[i, 0:5, :] = total[5 * i : 5 * i + 5, :]
    tc = {}
    for d in range(1, 2 * NY):
        tc[d] = rcopy(
            tsend.at[lax.rem(ctx + d, 2 * NY)], trecv.at[d], ts.at[d], tr.at[d], tdev[d]
        )
        tc[d].start()
    same = tsend[ctx]
    other = jnp.zeros((8, N), F32)
    for d in range(1, 2 * NY):
        tc[d].wait_recv()
        if d % 2 == 0:
            same = same + trecv[d]
        else:
            other = other + trecv[d]
    out_ref[:, :N] = jnp.where(first, same, other)[:5]
    out_ref[:, N:] = jnp.where(first, other, same)[:5]
    for group in (pc, xc, zc, tc):
        for one in group.values():
            one.wait_send()


VMEM = pl.BlockSpec(memory_space=pltpu.VMEM)
DMA = pltpu.SemaphoreType.DMA


def params(i):
    return pltpu.CompilerParams(collective_id=i, has_side_effects=True, vmem_limit_bytes=60 * 1024 * 1024)


def body(u_codes, u_scale, w_bc, xs, dt, log_keep, dy, lengths):
    v = pltpu.VMEM
    u, proj = pl.pallas_call(
        project_kernel,
        out_shape=(jax.ShapeDtypeStruct((CH, D), BF16), jax.ShapeDtypeStruct((CH, 2 * N), BF16)),
        in_specs=[VMEM] * 3,
        out_specs=(VMEM, VMEM),
        scratch_shapes=[v((D, 2 * N), BF16), DMA((NY,)), DMA((NY,)), DMA((NY,)), DMA((NY,)), DMA],
        compiler_params=params(0),
        name="project",
    )(u_codes[0], u_scale[0], w_bc)
    offset = lax.axis_index("ctx") * CH
    at = lengths[0, 0] - offset
    r_eff = jnp.where(at < 0, 1 << 20, at)
    r_end = jnp.where(r_eff < CH, r_eff, 0)
    limit = jnp.where(offset > 0, r_eff, 0)
    marks = jnp.stack([r_eff, r_end, limit]).astype(jnp.int32)
    hp = H * P_SIZE
    gdt, gkeep, dbc = pl.pallas_call(
        mixer_kernel,
        out_shape=(
            jax.ShapeDtypeStruct((H, CH), F32),
            jax.ShapeDtypeStruct((H, CH), F32),
            jax.ShapeDtypeStruct((CH, 2 * N), BF16),
        ),
        in_specs=[pl.BlockSpec(memory_space=pltpu.SMEM)] + [VMEM] * 5,
        out_specs=(VMEM,) * 3,
        scratch_shapes=[
            v((2, CH, hp), BF16), v((2, CH, hp), BF16), v((hp, N), F32), v((hp, N), F32),
            v((HALF, N), F32), v((HALF, N), F32),
            v((H, 128), F32), v((H, 128), F32),
            v((HALF, N), BF16), v((HALF, N), BF16), v((HALF, N), BF16), v((HALF, N), BF16),
            v((hp, N), F32), v((hp, N), F32), v((HALF, N), F32), v((HALF, N), F32),
            v((CH, 128), F32), v((H, CH), F32), v((CH, CH), F32), v((CH, CH), F32), v((CH, CH), F32),
            v((H, CH), F32), v((CH, 128), F32), v((CH, 128), F32), v((CH, 128), F32), v((CH, 128), F32),
            DMA((3,)), DMA((3,)),
        ] + [DMA((NCHUNK,))] * 8,
        compiler_params=params(1),
        name="mixer",
    )(marks, xs[0], dy[0], proj, dt[0], log_keep[0])
    span = D // NX
    grad = pl.pallas_call(
        reduce_kernel,
        out_shape=jax.ShapeDtypeStruct((5, 2 * N), F32),
        in_specs=[VMEM] * 2,
        out_specs=VMEM,
        scratch_shapes=[
            v((span, N), F32), v((NX, span, N), F32), v((NX, span, N), F32),
            v((NX, span, N), BF16), v((NX, span, N), BF16), v((span, N), F32),
            v((NZ, span // NZ, N), BF16), v((NZ, span // NZ, N), BF16),
            v((2 * NY, 8, N), F32), v((2 * NY, 8, N), F32),
            DMA((NX,)), DMA((NX,)), DMA((NX,)), DMA((NX,)), DMA((NZ,)), DMA((NZ,)),
            DMA((2 * NY,)), DMA((2 * NY,)),
        ],
        compiler_params=params(2),
        name="reduce",
    )(u, dbc)
    return grad, gdt[None], gkeep[None]


def solution(mesh):
    placed = (
        P("dp", "ctx", None),
        P("dp", "ctx", None),
        P("ctx", None),
        P("dp", "ctx", None),
        P("dp", None, "ctx"),
        P("dp", None, "ctx"),
        P("dp", "ctx", None),
        P("dp", None),
    )
    return jax.shard_map(
        body,
        mesh=mesh,
        in_specs=placed,
        out_specs=(P(("dp", "ctx"), None), P("dp", None, "ctx"), P("dp", None, "ctx")),
        check_vma=False,
    )
```

```python
import functools

import jax
import jax.numpy as jnp
from jax import lax
from jax.experimental import pallas as pl
from jax.experimental.pallas import tpu as pltpu
from jax.sharding import PartitionSpec as P

D = 2560
H = 40
P_SIZE = 64
N = 128
CH = 256
QB = 128
HALF = H * P_SIZE // 2
NY = 8
NX = 4
NZ = 8
ROWS_W = 160
CHUNK = 128
NCHUNK = HALF // CHUNK
SKEW = 4
SLOTS = max(NCHUNK + SKEW * (NY - 1), H // 2)
BLK = 512
F32 = jnp.float32
BF16 = jnp.bfloat16
MESH = pl.DeviceIdType.MESH
EXACT = lax.Precision.HIGHEST
NT = (((1,), (1,)), ((), ()))
TN = (((0,), (0,)), ((), ()))


def dot(a, b, dims=None, precision=None):
    if dims is None:
        dims = (((1,), (0,)), ((), ()))
    return lax.dot_general(a, b, dims, precision=precision, preferred_element_type=F32)


def split(v):
    hi = v.astype(BF16)
    return hi, (v - hi.astype(F32)).astype(BF16)


def dot2(pair, b, dims=None):
    return dot(pair[0], b, dims) + dot(pair[1], b, dims)


def where_am_i():
    dp = lax.axis_index("dp")
    ctx = lax.axis_index("ctx")
    return dp, ctx, lax.div(ctx, 2), lax.rem(ctx, 2)


def rcopy(src, dst, send, recv, dev):
    return pltpu.make_async_remote_copy(
        src_ref=src, dst_ref=dst, send_sem=send, recv_sem=recv, device_id=dev, device_id_type=MESH
    )


def iota(shape, dim):
    return lax.broadcasted_iota(jnp.int32, shape, dim)


def greet(peers):
    barrier = pltpu.get_barrier_semaphore()
    for dev in peers:
        pl.semaphore_signal(barrier, inc=1, device_id=dev, device_id_type=MESH)
    return barrier, len(peers)


def mixer_kernel(
    marks, codes_ref, scale_ref, w_ref, x_ref, dy_ref, dt_ref, keep_ref, grad_ref, gdt_ref, gkeep_ref,
    u_t, w_all, u_ref,
    dyw, xw, sloc, gloc, prt_s, prt_g, c_own, c_prt,
    fsend, frecv, vsend, vrecv, s_all, g_all, os, og,
    racc, cacc, ssum, bound, cross, cumr, cum_t, ds_t, de_t, dt_t,
    own, psend, precv, xsend, xrecv, zsum, zsend, zrecv, tsend, trecv,
    ws, wr, rs, rr, lsem,
    ps, pr, fs, fr, vs, vr, oss, osr, ogs, ogr,
    qs, qr, xs_, xr, zs, zr, ts, tr,
):
    dp, ctx, y, c = where_am_i()
    x, z = lax.div(dp, NZ), lax.rem(dp, NZ)
    partner = (dp, 2 * y + 1 - c)
    ahead = (dp, lax.rem(y + 1, NY) * 2 + c)
    behind = (dp, lax.rem(y + NY - 1, NY) * 2 + c)
    xdev = [(lax.rem(x + d, NX) * NZ + z, ctx) for d in range(NX)]
    zdev = [(x * NZ + lax.rem(z + d, NZ), ctx) for d in range(NZ)]
    tdev = [(dp, lax.rem(ctx + d, 2 * NY)) for d in range(2 * NY)]
    barrier, count = greet([xdev[1], xdev[3]] + zdev[1:] + tdev[1:])
    pl.semaphore_wait(barrier, count)
    r_eff, r_end, limit = marks[0], marks[1], marks[2]
    first = c == 0
    part_rows = ROWS_W // 2

    def w_rows(back, sub):
        owner = lax.rem(y + NY - back, NY) * 2 + c
        return pl.ds(pl.multiple_of(owner * ROWS_W + sub * part_rows, 16), part_rows)

    def w_copy(way, hop, sub):
        n = (way * 4 + hop - 1) * 2 + sub
        at = w_rows(hop - 1 if way == 0 else NY - hop + 1, sub)
        src = w_ref.at[sub * part_rows : (sub + 1) * part_rows] if hop == 1 else w_all.at[at]
        return rcopy(src, w_all.at[at], ws.at[n], wr.at[n], ahead if way == 0 else behind)

    def w_relay(way, hop, sub):
        n = (way * 4 + hop - 1) * 2 + sub
        at = w_rows(hop if way == 0 else NY - hop, sub)
        return rcopy(w_all.at[at], w_all.at[at], rs.at[n], rr.at[n], partner)

    messages = [(way, hop, sub) for hop in range(1, 5) for sub in range(2) for way in range(2) if hop < 4 or sub == way]
    copies = {m: w_copy(*m) for m in messages}
    relays = {m: w_relay(*m) for m in messages}
    for m in messages[:4]:
        copies[m].start()
    mine_w = pl.ds(pl.multiple_of(ctx * ROWS_W, 32), ROWS_W)
    own_relay = rcopy(w_ref, w_all.at[mine_w], rs.at[16], rr.at[16], partner)
    own_relay.start()
    local = pltpu.make_async_copy(w_ref, w_all.at[mine_w], lsem)
    local.start()

    pad = jnp.zeros((128 - H, CH), F32)
    row, col = iota((CH, CH), 0), iota((CH, CH), 1)
    scales = jnp.transpose(jnp.concatenate([scale_ref[...], jnp.zeros((128 - D // QB, CH), F32)], axis=0))

    def dequantize(n):
        for j in range(2 * n, 2 * n + 2):
            at = slice(j * QB, (j + 1) * QB)
            u_ref[:, at] = (codes_ref[:, at].astype(F32) * scales[:, j : j + 1]).astype(BF16)
            u_t[at, :] = jnp.transpose(u_ref[:, at])

    def decays():
        same = jnp.where(row >= r_eff, 1, 0) == jnp.where(col >= r_eff, 1, 0)
        bound[...] = jnp.where((col <= row) & same, 0.0, -1e30)
        upto = jnp.where(row <= col, 1.0, 0.0)
        keep_p = jnp.concatenate([keep_ref[...], pad], axis=0)
        cum_p = dot(keep_p, upto, precision=EXACT)
        cumr[...] = cum_p[:H]
        cum = jnp.transpose(cum_p)
        cum_t[...] = cum
        dts = jnp.transpose(jnp.concatenate([dt_ref[...], pad], axis=0))
        tcol = iota((CH, 128), 0)
        ds = jnp.where(tcol < limit, jnp.exp(cum), 0.0)
        de = jnp.where(tcol >= r_end, jnp.exp(cum[CH - 1 : CH, :] - cum), 0.0)
        ds_t[...] = ds
        de_t[...] = de
        dt_t[...] = dts
        carry = jnp.where(CH - 1 < limit, jnp.exp(cum_p[:H, CH - 1 : CH]), 0.0)
        c_own[...] = jnp.broadcast_to(carry, (H, 128))
        ssum[...] = jnp.zeros_like(ssum)
        racc[...] = jnp.zeros_like(racc)

    def weigh(g):
        at = slice(g * BLK, (g + 1) * BLK)
        head = lax.rem(iota((CH, BLK), 0), 128)
        spread = jnp.where(head == 8 * g + lax.div(iota((CH, BLK), 1), P_SIZE), 1.0, 0.0).astype(BF16)
        ds_hl = jnp.concatenate(split(ds_t[...]), axis=1)
        ws_hl = jnp.concatenate(split(de_t[...] * dt_t[...]), axis=1)
        dyb = split(dy_ref[:, at].astype(F32) * dot(ds_hl, spread))
        xb = split(x_ref[:, at].astype(F32) * dot(ws_hl, spread))
        for n in range(2):
            dyw[n, :, at] = dyb[n]
            xw[n, :, at] = xb[n]

    work = [functools.partial(dequantize, n) for n in range(10)]
    work += [decays] + [functools.partial(weigh, g) for g in range(5)]
    for n, m in enumerate(messages):
        if n % 2 == 0:
            for _ in range(2):
                if work:
                    work.pop(0)()
        way, hop, sub = m
        copies[m].wait_recv()
        onward = (way, hop + 1, sub)
        if onward in copies:
            copies[onward].start()
        relays[m].start()
    while work:
        work.pop(0)()
    local.wait()
    own_relay.wait_recv()
    for m in messages:
        relays[m].wait_recv()
    proj = dot(u_ref[...], w_all[...]).astype(BF16)
    b_mat, c_mat = proj[:, :N], proj[:, N:]

    mine = pl.multiple_of(c * HALF, 128)
    other_half = pl.multiple_of((1 - c) * HALF, 128)
    theirs = pl.ds(other_half, HALF)

    def local_states(base):
        def step(g, _):
            at = pl.ds(pl.multiple_of(base + g * 256, 128), 256)
            sloc[at, :] = dot2((xw[0, :, at], xw[1, :, at]), b_mat, TN)
            gloc[at, :] = dot2((dyw[0, :, at], dyw[1, :, at]), c_mat, TN)
            return 0

        lax.fori_loop(0, HALF // 256, step, 0)

    local_states(other_half)
    swap = [
        rcopy(c_own, c_prt, ps.at[0], pr.at[0], partner),
        rcopy(sloc.at[theirs], prt_s, ps.at[1], pr.at[1], partner),
        rcopy(gloc.at[theirs], prt_g, ps.at[2], pr.at[2], partner),
    ]
    for one in swap:
        one.start()
    local_states(mine)
    cross[...] = dot(c_mat, b_mat, NT)
    lane = iota((CH, 128), 1)

    @pl.when(y == 0)
    def _():
        frecv[...] = jnp.zeros_like(frecv)

    @pl.when(y == NY - 1)
    def _():
        vrecv[...] = jnp.zeros_like(vrecv)


    def chunk_rows(i):
        return pl.ds(pl.multiple_of(i * CHUNK, CHUNK), CHUNK)

    def decay(ref, i):
        h = c * (H // 2) + 2 * i
        return jnp.concatenate(
            [jnp.broadcast_to(ref[pl.ds(h + j, 1), :], (P_SIZE, N)) for j in range(2)], axis=0
        )

    def pick(i, own, other):
        a = own[pl.ds(pl.multiple_of(mine + i * CHUNK, CHUNK), CHUNK), :]
        b = other[chunk_rows(i), :]
        return jnp.where(first, a, b), jnp.where(first, b, a)

    def f_copy(i):
        return rcopy(fsend.at[chunk_rows(i)], frecv.at[chunk_rows(i)], fs.at[i], fr.at[i], ahead)

    def v_copy(i):
        return rcopy(vsend.at[chunk_rows(i)], vrecv.at[chunk_rows(i)], vs.at[i], vr.at[i], behind)

    def full_rows(i):
        return pl.ds(pl.multiple_of(mine + i * CHUNK, CHUNK), CHUNK)

    def s_copy(i):
        return rcopy(os.at[chunk_rows(i)], s_all.at[full_rows(i)], oss.at[i], osr.at[i], partner)

    def g_copy(i):
        return rcopy(og.at[chunk_rows(i)], g_all.at[full_rows(i)], ogs.at[i], ogr.at[i], partner)

    def slot(k, _):
        @pl.when(k < H // 2)
        def _():
            at = pl.ds(pl.multiple_of(k * 128, 128), 128)
            x2, dy2 = x_ref[:, at], dy_ref[:, at]
            turned = pltpu.roll(cum_t[...], lax.rem(128 - 2 * k, 128), 1)
            for j in range(2):
                h = 2 * k + j
                xm = jnp.where((lane < P_SIZE) if j == 0 else (lane >= P_SIZE), x2, jnp.zeros_like(x2))
                dots = dot(dy2, xm, NT)
                diff = turned[:, j : j + 1] - cumr[pl.ds(h, 1), :]
                mixed = jnp.exp(jnp.minimum(diff, bound[...])) * dots
                pair = mixed * cross[...]
                steps = dt_ref[pl.ds(h, 1), :]
                ssum[...] += mixed * steps
                cacc[pl.ds(h, 1), :] = jnp.sum(pair, axis=0, keepdims=True)
                rsum = jnp.sum(pair * steps, axis=1, keepdims=True)
                racc[...] += jnp.where(lane == h, rsum, 0.0)

        @pl.when(k == 0)
        def _():
            for one in swap:
                one.wait_recv()

        i = k - SKEW * y

        @pl.when((i >= 0) & (i < NCHUNK))
        def _():
            @pl.when(y > 0)
            def _():
                f_copy(i).wait_recv()

            a0, a1 = decay(c_own, i), decay(c_prt, i)
            a0, a1 = jnp.where(first, a0, a1), jnp.where(first, a1, a0)
            s0, s1 = pick(i, sloc, prt_s)
            state = frecv[chunk_rows(i), :].astype(F32)
            mid = a0 * state + s0

            @pl.when(y < NY - 1)
            def _():
                fsend[chunk_rows(i), :] = (a1 * mid + s1).astype(BF16)
                f_copy(i).start()

            os[chunk_rows(i), :] = jnp.where(first, mid, state)
            s_copy(i).start()
            s_all[full_rows(i), :] = jnp.where(first, state, mid)

        q = k - SKEW * (NY - 1 - y)

        @pl.when((q >= 0) & (q < NCHUNK))
        def _():
            @pl.when(y < NY - 1)
            def _():
                v_copy(q).wait_recv()

            a0, a1 = decay(c_own, q), decay(c_prt, q)
            a0, a1 = jnp.where(first, a0, a1), jnp.where(first, a1, a0)
            g0, g1 = pick(q, gloc, prt_g)
            state = vrecv[chunk_rows(q), :].astype(F32)
            mid = a1 * state + g1

            @pl.when(y > 0)
            def _():
                vsend[chunk_rows(q), :] = (a0 * mid + g0).astype(BF16)
                v_copy(q).start()

            og[chunk_rows(q), :] = jnp.where(first, state, mid)
            g_copy(q).start()
            g_all[full_rows(q), :] = jnp.where(first, mid, state)

        return 0

    lax.fori_loop(0, SLOTS, slot, 0)

    def drain(i, _):
        s_copy(i).wait()
        g_copy(i).wait()

        @pl.when(y < NY - 1)
        def _():
            f_copy(i).wait_send()

        @pl.when(y > 0)
        def _():
            v_copy(i).wait_send()

        return 0

    lax.fori_loop(0, NCHUNK, drain, 0)

    def outer(g, sums):
        x_t, e_t, gc, gb_, const = sums
        at = pl.ds(pl.multiple_of(g * BLK, BLK), BLK)
        s_blk, g_blk = s_all[at, :], g_all[at, :]
        gather = jnp.where(8 * g + lax.div(iota((BLK, 128), 0), P_SIZE) == iota((BLK, 128), 1), 1.0, 0.0).astype(BF16)
        fold = jnp.where(8 * g + lax.div(iota((128, BLK), 1), P_SIZE) == iota((128, BLK), 0), 1.0, 0.0).astype(BF16)
        both = split(s_blk * g_blk)
        s_blk, g_blk = split(s_blk), split(g_blk)
        inner_y = dot(c_mat, s_blk[0], NT) + dot(c_mat, s_blk[1], NT)
        inner_x = dot(b_mat, g_blk[0], NT) + dot(b_mat, g_blk[1], NT)
        prod_y = split(dy_ref[:, at].astype(F32) * inner_y)
        prod_x = split(x_ref[:, at].astype(F32) * inner_x)
        return (
            x_t + dot2(prod_y, gather),
            e_t + dot2(prod_x, gather),
            gc + dot2((dyw[0, :, at], dyw[1, :, at]), s_blk[0]) + dot(dyw[0, :, at], s_blk[1]),
            gb_ + dot2((xw[0, :, at], xw[1, :, at]), g_blk[0]) + dot(xw[0, :, at], g_blk[1]),
            const + dot(fold, both[0]) + dot(fold, both[1]),
        )

    sums = split(ssum[...])
    zero = jnp.zeros((CH, 128), F32)
    start = (zero, zero, dot2(sums, b_mat), dot2(sums, c_mat, TN), jnp.zeros((128, 128), F32))
    x_t, e_t, gc, gb_, const = lax.fori_loop(0, H * P_SIZE // BLK, outer, start)

    d_b, d_c = gb_.astype(BF16), gc.astype(BF16)
    d_own = jnp.where(first, d_b, d_c)
    d_oth = jnp.where(first, d_c, d_b)
    span = D // NX
    piece = span // NZ
    half = span // 2
    order = (2, 1, 3, 0)

    def u_rows(d):
        return u_t[pl.ds(pl.multiple_of(lax.rem(x + d, NX) * span, 128), span), :]

    pc = {}
    for d in order:
        psend[d] = dot(u_rows(d), d_oth)
        pc[d] = rcopy(psend.at[d], precv.at[d], qs.at[d], qr.at[d], partner)
        pc[d].start()
    xc = {}

    def x_send(n, value, d):
        xsend[n] = value.astype(BF16)
        xc[n] = rcopy(xsend.at[n], xrecv.at[n], xs_.at[n], xr.at[n], xdev[d])
        xc[n].start()

    for d in order:
        part = dot(u_rows(d), d_own)
        pc[d].wait_recv()
        own[d] = part + precv[d]
        if d == 2:
            x_send(0, own[2, :half], 1)
            x_send(1, own[2, half:], 3)
        if d == 1:
            x_send(2, own[1, half:], 1)
        if d == 3:
            x_send(3, own[3, :half], 3)
    xc[0].wait_recv()
    x_send(4, own[1, :half] + xrecv[0].astype(F32), 1)
    xc[1].wait_recv()
    x_send(5, own[3, half:] + xrecv[1].astype(F32), 3)

    ext_t = e_t * de_t[...]
    ext = jnp.transpose(ext_t)[:H]
    zed = jnp.transpose(ext_t * dt_t[...])[:H]
    late = jnp.transpose(x_t * ds_t[...] + racc[...])[:H]
    gdt_ref[...] = cacc[...] + ext
    since = jnp.where(row >= col, 1.0, 0.0)
    before = jnp.where(row < col, 1.0, 0.0)
    fixed = jnp.sum(const, axis=1, keepdims=True)[:H] * c_own[:, :1]
    gkeep_ref[...] = (
        dot(late - cacc[...] * dt_ref[...], since, precision=EXACT) + dot(zed, before, precision=EXACT) + fixed
    )

    for n in range(2, 6):
        xc[n].wait_recv()
    zsum[:half] = own[0, :half] + xrecv[4].astype(F32) + xrecv[3].astype(F32)
    zsum[half:] = own[0, half:] + xrecv[2].astype(F32) + xrecv[5].astype(F32)
    zc = {}
    for d in (4, 3, 5, 2, 6, 1, 7):
        at = pl.ds(pl.multiple_of(lax.rem(z + d, NZ) * piece, 16), piece)
        zsend[d] = zsum[at, :].astype(BF16)
        zc[d] = rcopy(zsend.at[d], zrecv.at[d], zs.at[d], zr.at[d], zdev[d])
        zc[d].start()
    total = zsum[pl.ds(pl.multiple_of(z * piece, 16), piece), :]
    for d in (1, 7, 2, 6, 3, 5, 4):
        zc[d].wait_recv()
        total = total + zrecv[d].astype(F32)
    tsend[...] = jnp.zeros_like(tsend)
    for i in range(2 * NY):
        tsend[i, 0:5, :] = total[5 * i : 5 * i + 5, :]
    tc = {}
    for d in range(1, 2 * NY):
        tc[d] = rcopy(
            tsend.at[lax.rem(ctx + d, 2 * NY)], trecv.at[d], ts.at[d], tr.at[d], tdev[d]
        )
        tc[d].start()
    same_core = tsend[ctx]
    other_core = jnp.zeros((8, N), F32)
    for d in range(1, 2 * NY):
        tc[d].wait_recv()
        if d % 2 == 0:
            same_core = same_core + trecv[d]
        else:
            other_core = other_core + trecv[d]
    grad_ref[:, :N] = jnp.where(first, same_core, other_core)[:5]
    grad_ref[:, N:] = jnp.where(first, other_core, same_core)[:5]
    for group in (copies, relays, pc, xc, zc, tc):
        for one in group.values():
            one.wait_send()
    own_relay.wait_send()
    for one in swap:
        one.wait_send()


VMEM = pl.BlockSpec(memory_space=pltpu.VMEM)
DMA = pltpu.SemaphoreType.DMA


def body(u_codes, u_scale, w_bc, xs, dt, log_keep, dy, lengths):
    v = pltpu.VMEM
    offset = lax.axis_index("ctx") * CH
    at = lengths[0, 0] - offset
    r_eff = jnp.where(at < 0, 1 << 20, at)
    r_end = jnp.where(r_eff < CH, r_eff, 0)
    limit = jnp.where(offset > 0, r_eff, 0)
    marks = jnp.stack([r_eff, r_end, limit]).astype(jnp.int32)
    hp = H * P_SIZE
    span = D // NX
    grad, gdt, gkeep = pl.pallas_call(
        mixer_kernel,
        out_shape=(
            jax.ShapeDtypeStruct((5, 2 * N), F32),
            jax.ShapeDtypeStruct((H, CH), F32),
            jax.ShapeDtypeStruct((H, CH), F32),
        ),
        in_specs=[pl.BlockSpec(memory_space=pltpu.SMEM)] + [VMEM] * 7,
        out_specs=(VMEM,) * 3,
        scratch_shapes=[
            v((D, CH), BF16), v((D, 2 * N), BF16), v((CH, D), BF16),
            v((2, CH, hp), BF16), v((2, CH, hp), BF16), v((hp, N), F32), v((hp, N), F32),
            v((HALF, N), F32), v((HALF, N), F32),
            v((H, 128), F32), v((H, 128), F32),
            v((HALF, N), BF16), v((HALF, N), BF16), v((HALF, N), BF16), v((HALF, N), BF16),
            v((hp, N), F32), v((hp, N), F32), v((HALF, N), F32), v((HALF, N), F32),
            v((CH, 128), F32), v((H, CH), F32), v((CH, CH), F32), v((CH, CH), F32), v((CH, CH), F32),
            v((H, CH), F32), v((CH, 128), F32), v((CH, 128), F32), v((CH, 128), F32), v((CH, 128), F32),
            v((NX, span, N), F32), v((NX, span, N), F32), v((NX, span, N), F32),
            v((6, span // 2, N), BF16), v((6, span // 2, N), BF16), v((span, N), F32),
            v((NZ, span // NZ, N), BF16), v((NZ, span // NZ, N), BF16),
            v((2 * NY, 8, N), F32), v((2 * NY, 8, N), F32),
            DMA((16,)), DMA((16,)), DMA((17,)), DMA((17,)), DMA,
            DMA((3,)), DMA((3,)),
        ] + [DMA((NCHUNK,))] * 8 + [
            DMA((NX,)), DMA((NX,)), DMA((6,)), DMA((6,)), DMA((NZ,)), DMA((NZ,)),
            DMA((2 * NY,)), DMA((2 * NY,)),
        ],
        compiler_params=pltpu.CompilerParams(
            collective_id=0, has_side_effects=True, vmem_limit_bytes=60 * 1024 * 1024
        ),
        name="mixer",
    )(marks, u_codes[0], u_scale[0].T, w_bc, xs[0], dy[0], dt[0], log_keep[0])
    return grad, gdt[None], gkeep[None]


def solution(mesh):
    placed = (
        P("dp", "ctx", None),
        P("dp", "ctx", None),
        P("ctx", None),
        P("dp", "ctx", None),
        P("dp", None, "ctx"),
        P("dp", None, "ctx"),
        P("dp", "ctx", None),
        P("dp", None),
    )
    return jax.shard_map(
        body,
        mesh=mesh,
        in_specs=placed,
        out_specs=(P(("dp", "ctx"), None), P("dp", None, "ctx"), P("dp", None, "ctx")),
        check_vma=False,
    )
```

```python
import functools

import jax
import jax.numpy as jnp
from jax import lax
from jax.experimental import pallas as pl
from jax.experimental.pallas import tpu as pltpu
from jax.sharding import PartitionSpec as P

D = 2560
H = 40
P_SIZE = 64
N = 128
CH = 256
QB = 128
HALF = H * P_SIZE // 2
NY = 8
NX = 4
NZ = 8
ROWS_W = 160
CHUNK = 128
NCHUNK = HALF // CHUNK
SKEW = 6
SLOTS = max(NCHUNK + SKEW * (NY - 1), H // 2)
BLK = 512
F32 = jnp.float32
BF16 = jnp.bfloat16
MESH = pl.DeviceIdType.MESH
EXACT = lax.Precision.HIGHEST
NT = (((1,), (1,)), ((), ()))
TN = (((0,), (0,)), ((), ()))


def dot(a, b, dims=None, precision=None):
    if dims is None:
        dims = (((1,), (0,)), ((), ()))
    return lax.dot_general(a, b, dims, precision=precision, preferred_element_type=F32)


def split(v):
    hi = v.astype(BF16)
    return hi, (v - hi.astype(F32)).astype(BF16)


def dot2(pair, b, dims=None):
    return dot(pair[0], b, dims) + dot(pair[1], b, dims)


def where_am_i():
    dp = lax.axis_index("dp")
    ctx = lax.axis_index("ctx")
    return dp, ctx, lax.div(ctx, 2), lax.rem(ctx, 2)


def rcopy(src, dst, send, recv, dev):
    return pltpu.make_async_remote_copy(
        src_ref=src, dst_ref=dst, send_sem=send, recv_sem=recv, device_id=dev, device_id_type=MESH
    )


def iota(shape, dim):
    return lax.broadcasted_iota(jnp.int32, shape, dim)


def greet(peers):
    barrier = pltpu.get_barrier_semaphore()
    for dev in peers:
        pl.semaphore_signal(barrier, inc=1, device_id=dev, device_id_type=MESH)
    return barrier, len(peers)


def mixer_kernel(
    marks, codes_ref, scale_ref, w_ref, x_ref, dy_ref, dt_ref, keep_ref, grad_ref, gdt_ref, gkeep_ref,
    u_t, w_all, u_ref,
    dyw, xw, sloc, gloc, prt_s, prt_g, c_own, c_prt,
    fsend, frecv, vsend, vrecv, s_all, g_all, os, og,
    racc, cacc, ssum, bound, cross, cumr, cum_t, ds_t, de_t, dt_t,
    own, psend, precv, xsend, xrecv, zsum, zsend, zrecv, tsend, trecv,
    ws, wr, rs, rr, lsem,
    ps, pr, fs, fr, vs, vr, oss, osr, ogs, ogr,
    qs, qr, xs_, xr, zs, zr, ts, tr,
):
    dp, ctx, y, c = where_am_i()
    x, z = lax.div(dp, NZ), lax.rem(dp, NZ)
    partner = (dp, 2 * y + 1 - c)
    ahead = (dp, lax.rem(y + 1, NY) * 2 + c)
    behind = (dp, lax.rem(y + NY - 1, NY) * 2 + c)
    xdev = [(lax.rem(x + d, NX) * NZ + z, ctx) for d in range(NX)]
    zdev = [(x * NZ + lax.rem(z + d, NZ), ctx) for d in range(NZ)]
    tdev = [(dp, lax.rem(ctx + d, 2 * NY)) for d in range(2 * NY)]
    barrier, count = greet([xdev[1], xdev[3]] + zdev[1:] + tdev[1:])
    pl.semaphore_wait(barrier, count)
    r_eff, r_end, limit = marks[0], marks[1], marks[2]
    first = c == 0
    part_rows = ROWS_W // 2

    def w_rows(back, sub):
        owner = lax.rem(y + NY - back, NY) * 2 + c
        return pl.ds(pl.multiple_of(owner * ROWS_W + sub * part_rows, 16), part_rows)

    def w_copy(way, hop, sub):
        n = (way * 4 + hop - 1) * 2 + sub
        at = w_rows(hop - 1 if way == 0 else NY - hop + 1, sub)
        src = w_ref.at[sub * part_rows : (sub + 1) * part_rows] if hop == 1 else w_all.at[at]
        return rcopy(src, w_all.at[at], ws.at[n], wr.at[n], ahead if way == 0 else behind)

    def w_relay(way, hop, sub):
        n = (way * 4 + hop - 1) * 2 + sub
        at = w_rows(hop if way == 0 else NY - hop, sub)
        return rcopy(w_all.at[at], w_all.at[at], rs.at[n], rr.at[n], partner)

    messages = [(way, hop, sub) for hop in range(1, 5) for sub in range(2) for way in range(2) if hop < 4 or sub == way]
    copies = {m: w_copy(*m) for m in messages}
    relays = {m: w_relay(*m) for m in messages}
    for m in messages[:4]:
        copies[m].start()
    mine_w = pl.ds(pl.multiple_of(ctx * ROWS_W, 32), ROWS_W)
    own_relay = rcopy(w_ref, w_all.at[mine_w], rs.at[16], rr.at[16], partner)
    own_relay.start()
    local = pltpu.make_async_copy(w_ref, w_all.at[mine_w], lsem)
    local.start()

    pad = jnp.zeros((128 - H, CH), F32)
    row, col = iota((CH, CH), 0), iota((CH, CH), 1)
    scales = jnp.transpose(jnp.concatenate([scale_ref[...], jnp.zeros((128 - D // QB, CH), F32)], axis=0))

    def dequantize(n):
        for j in range(2 * n, 2 * n + 2):
            at = slice(j * QB, (j + 1) * QB)
            u_ref[:, at] = (codes_ref[:, at].astype(F32) * scales[:, j : j + 1]).astype(BF16)
            u_t[at, :] = jnp.transpose(u_ref[:, at])

    def decays():
        same = jnp.where(row >= r_eff, 1, 0) == jnp.where(col >= r_eff, 1, 0)
        bound[...] = jnp.where((col <= row) & same, 0.0, -1e30)
        upto = jnp.where(row <= col, 1.0, 0.0)
        keep_p = jnp.concatenate([keep_ref[...], pad], axis=0)
        cum_p = dot(keep_p, upto, precision=EXACT)
        cumr[...] = cum_p[:H]
        cum = jnp.transpose(cum_p)
        cum_t[...] = cum
        dts = jnp.transpose(jnp.concatenate([dt_ref[...], pad], axis=0))
        tcol = iota((CH, 128), 0)
        ds = jnp.where(tcol < limit, jnp.exp(cum), 0.0)
        de = jnp.where(tcol >= r_end, jnp.exp(cum[CH - 1 : CH, :] - cum), 0.0)
        ds_t[...] = ds
        de_t[...] = de
        dt_t[...] = dts
        carry = jnp.where(CH - 1 < limit, jnp.exp(cum_p[:H, CH - 1 : CH]), 0.0)
        c_own[...] = jnp.broadcast_to(carry, (H, 128))
        ssum[...] = jnp.zeros_like(ssum)
        racc[...] = jnp.zeros_like(racc)

    def weigh(g):
        at = slice(g * BLK, (g + 1) * BLK)
        head = lax.rem(iota((CH, BLK), 0), 128)
        spread = jnp.where(head == 8 * g + lax.div(iota((CH, BLK), 1), P_SIZE), 1.0, 0.0).astype(BF16)
        ds_hl = jnp.concatenate(split(ds_t[...]), axis=1)
        ws_hl = jnp.concatenate(split(de_t[...] * dt_t[...]), axis=1)
        dyb = split(dy_ref[:, at].astype(F32) * dot(ds_hl, spread))
        xb = split(x_ref[:, at].astype(F32) * dot(ws_hl, spread))
        for n in range(2):
            dyw[n, :, at] = dyb[n]
            xw[n, :, at] = xb[n]

    work = [functools.partial(dequantize, n) for n in range(10)]
    work += [decays] + [functools.partial(weigh, g) for g in range(5)]
    for n, m in enumerate(messages):
        if n % 2 == 0:
            for _ in range(2):
                if work:
                    work.pop(0)()
        way, hop, sub = m
        copies[m].wait_recv()
        onward = (way, hop + 1, sub)
        if onward in copies:
            copies[onward].start()
        relays[m].start()
    while work:
        work.pop(0)()
    local.wait()
    own_relay.wait_recv()
    for m in messages:
        relays[m].wait_recv()
    proj = dot(u_ref[...], w_all[...]).astype(BF16)
    b_mat, c_mat = proj[:, :N], proj[:, N:]

    mine = pl.multiple_of(c * HALF, 128)
    other_half = pl.multiple_of((1 - c) * HALF, 128)
    theirs = pl.ds(other_half, HALF)

    def local_states(base):
        def step(g, _):
            at = pl.ds(pl.multiple_of(base + g * 256, 128), 256)
            sloc[at, :] = dot2((xw[0, :, at], xw[1, :, at]), b_mat, TN)
            gloc[at, :] = dot2((dyw[0, :, at], dyw[1, :, at]), c_mat, TN)
            return 0

        lax.fori_loop(0, HALF // 256, step, 0)

    local_states(other_half)
    swap = [
        rcopy(c_own, c_prt, ps.at[0], pr.at[0], partner),
        rcopy(sloc.at[theirs], prt_s, ps.at[1], pr.at[1], partner),
        rcopy(gloc.at[theirs], prt_g, ps.at[2], pr.at[2], partner),
    ]
    for one in swap:
        one.start()
    local_states(mine)
    cross[...] = dot(c_mat, b_mat, NT)
    lane = iota((CH, 128), 1)

    @pl.when(y == 0)
    def _():
        frecv[...] = jnp.zeros_like(frecv)

    @pl.when(y == NY - 1)
    def _():
        vrecv[...] = jnp.zeros_like(vrecv)


    def chunk_rows(i):
        return pl.ds(pl.multiple_of(i * CHUNK, CHUNK), CHUNK)

    def decay(ref, i):
        h = c * (H // 2) + 2 * i
        return jnp.concatenate(
            [jnp.broadcast_to(ref[pl.ds(h + j, 1), :], (P_SIZE, N)) for j in range(2)], axis=0
        )

    def pick(i, own, other):
        a = own[pl.ds(pl.multiple_of(mine + i * CHUNK, CHUNK), CHUNK), :]
        b = other[chunk_rows(i), :]
        return jnp.where(first, a, b), jnp.where(first, b, a)

    def f_copy(i):
        return rcopy(fsend.at[chunk_rows(i)], frecv.at[chunk_rows(i)], fs.at[i], fr.at[i], ahead)

    def v_copy(i):
        return rcopy(vsend.at[chunk_rows(i)], vrecv.at[chunk_rows(i)], vs.at[i], vr.at[i], behind)

    def full_rows(i):
        return pl.ds(pl.multiple_of(mine + i * CHUNK, CHUNK), CHUNK)

    def s_copy(i):
        return rcopy(os.at[chunk_rows(i)], s_all.at[full_rows(i)], oss.at[i], osr.at[i], partner)

    def g_copy(i):
        return rcopy(og.at[chunk_rows(i)], g_all.at[full_rows(i)], ogs.at[i], ogr.at[i], partner)

    def slot(k, _):
        @pl.when(k < H // 2)
        def _():
            at = pl.ds(pl.multiple_of(k * 128, 128), 128)
            x2, dy2 = x_ref[:, at], dy_ref[:, at]
            turned = pltpu.roll(cum_t[...], lax.rem(128 - 2 * k, 128), 1)
            for j in range(2):
                h = 2 * k + j
                xm = jnp.where((lane < P_SIZE) if j == 0 else (lane >= P_SIZE), x2, jnp.zeros_like(x2))
                dots = dot(dy2, xm, NT)
                diff = turned[:, j : j + 1] - cumr[pl.ds(h, 1), :]
                mixed = jnp.exp(jnp.minimum(diff, bound[...])) * dots
                pair = mixed * cross[...]
                steps = dt_ref[pl.ds(h, 1), :]
                ssum[...] += mixed * steps
                cacc[pl.ds(h, 1), :] = jnp.sum(pair, axis=0, keepdims=True)
                rsum = jnp.sum(pair * steps, axis=1, keepdims=True)
                racc[...] += jnp.where(lane == h, rsum, 0.0)

        @pl.when(k == 0)
        def _():
            for one in swap:
                one.wait_recv()

        i = k - SKEW * y

        @pl.when((i >= 0) & (i < NCHUNK))
        def _():
            @pl.when(y > 0)
            def _():
                f_copy(i).wait_recv()

            a0, a1 = decay(c_own, i), decay(c_prt, i)
            a0, a1 = jnp.where(first, a0, a1), jnp.where(first, a1, a0)
            s0, s1 = pick(i, sloc, prt_s)
            state = frecv[chunk_rows(i), :].astype(F32)
            mid = a0 * state + s0

            @pl.when(y < NY - 1)
            def _():
                fsend[chunk_rows(i), :] = (a1 * mid + s1).astype(BF16)
                f_copy(i).start()

            os[chunk_rows(i), :] = jnp.where(first, mid, state)
            s_copy(i).start()
            s_all[full_rows(i), :] = jnp.where(first, state, mid)

        q = k - SKEW * (NY - 1 - y)

        @pl.when((q >= 0) & (q < NCHUNK))
        def _():
            @pl.when(y < NY - 1)
            def _():
                v_copy(q).wait_recv()

            a0, a1 = decay(c_own, q), decay(c_prt, q)
            a0, a1 = jnp.where(first, a0, a1), jnp.where(first, a1, a0)
            g0, g1 = pick(q, gloc, prt_g)
            state = vrecv[chunk_rows(q), :].astype(F32)
            mid = a1 * state + g1

            @pl.when(y > 0)
            def _():
                vsend[chunk_rows(q), :] = (a0 * mid + g0).astype(BF16)
                v_copy(q).start()

            og[chunk_rows(q), :] = jnp.where(first, state, mid)
            g_copy(q).start()
            g_all[full_rows(q), :] = jnp.where(first, mid, state)

        return 0

    lax.fori_loop(0, SLOTS, slot, 0)

    def drain(i, _):
        s_copy(i).wait()
        g_copy(i).wait()

        @pl.when(y < NY - 1)
        def _():
            f_copy(i).wait_send()

        @pl.when(y > 0)
        def _():
            v_copy(i).wait_send()

        return 0

    lax.fori_loop(0, NCHUNK, drain, 0)

    def outer(g, sums):
        x_t, e_t, gc, gb_, const = sums
        at = pl.ds(pl.multiple_of(g * BLK, BLK), BLK)
        s_blk, g_blk = s_all[at, :], g_all[at, :]
        gather = jnp.where(8 * g + lax.div(iota((BLK, 128), 0), P_SIZE) == iota((BLK, 128), 1), 1.0, 0.0).astype(BF16)
        fold = jnp.where(8 * g + lax.div(iota((128, BLK), 1), P_SIZE) == iota((128, BLK), 0), 1.0, 0.0).astype(BF16)
        both = split(s_blk * g_blk)
        s_blk, g_blk = split(s_blk), split(g_blk)
        inner_y = dot(c_mat, s_blk[0], NT) + dot(c_mat, s_blk[1], NT)
        inner_x = dot(b_mat, g_blk[0], NT) + dot(b_mat, g_blk[1], NT)
        prod_y = split(dy_ref[:, at].astype(F32) * inner_y)
        prod_x = split(x_ref[:, at].astype(F32) * inner_x)
        return (
            x_t + dot2(prod_y, gather),
            e_t + dot2(prod_x, gather),
            gc + dot2((dyw[0, :, at], dyw[1, :, at]), s_blk[0]) + dot(dyw[0, :, at], s_blk[1]),
            gb_ + dot2((xw[0, :, at], xw[1, :, at]), g_blk[0]) + dot(xw[0, :, at], g_blk[1]),
            const + dot(fold, both[0]) + dot(fold, both[1]),
        )

    sums = split(ssum[...])
    zero = jnp.zeros((CH, 128), F32)
    start = (zero, zero, dot2(sums, b_mat), dot2(sums, c_mat, TN), jnp.zeros((128, 128), F32))
    x_t, e_t, gc, gb_, const = lax.fori_loop(0, H * P_SIZE // BLK, outer, start)

    d_b, d_c = gb_.astype(BF16), gc.astype(BF16)
    d_both = jnp.concatenate([jnp.where(first, d_c, d_b), jnp.where(first, d_b, d_c)], axis=1)
    span = D // NX
    piece = span // NZ
    half = span // 2
    order = (2, 1, 3, 0)

    def u_rows(d):
        return u_t[pl.ds(pl.multiple_of(lax.rem(x + d, NX) * span, 128), span), :]

    pc = {}
    for d in order:
        product = dot(u_rows(d), d_both)
        psend[d] = product[:, :N]
        own[d] = product[:, N:]
        pc[d] = rcopy(psend.at[d], precv.at[d], qs.at[d], qr.at[d], partner)
        pc[d].start()
    xc = {}

    def x_send(n, value, d):
        xsend[n] = value.astype(BF16)
        xc[n] = rcopy(xsend.at[n], xrecv.at[n], xs_.at[n], xr.at[n], xdev[d])
        xc[n].start()

    for d in order:
        pc[d].wait_recv()
        own[d] += precv[d]
        if d == 2:
            x_send(0, own[2, :half], 1)
            x_send(1, own[2, half:], 3)
        if d == 1:
            x_send(2, own[1, half:], 1)
        if d == 3:
            x_send(3, own[3, :half], 3)
    xc[0].wait_recv()
    x_send(4, own[1, :half] + xrecv[0].astype(F32), 1)
    xc[1].wait_recv()
    x_send(5, own[3, half:] + xrecv[1].astype(F32), 3)

    ext_t = e_t * de_t[...]
    ext = jnp.transpose(ext_t)[:H]
    zed = jnp.transpose(ext_t * dt_t[...])[:H]
    late = jnp.transpose(x_t * ds_t[...] + racc[...])[:H]
    gdt_ref[...] = cacc[...] + ext
    since = jnp.where(row >= col, 1.0, 0.0)
    before = jnp.where(row < col, 1.0, 0.0)
    fixed = jnp.sum(const, axis=1, keepdims=True)[:H] * c_own[:, :1]
    gkeep_ref[...] = (
        dot(late - cacc[...] * dt_ref[...], since, precision=EXACT) + dot(zed, before, precision=EXACT) + fixed
    )

    for n in range(2, 6):
        xc[n].wait_recv()
    zsum[:half] = own[0, :half] + xrecv[4].astype(F32) + xrecv[3].astype(F32)
    zsum[half:] = own[0, half:] + xrecv[2].astype(F32) + xrecv[5].astype(F32)
    zc = {}
    for d in (4, 3, 5, 2, 6, 1, 7):
        at = pl.ds(pl.multiple_of(lax.rem(z + d, NZ) * piece, 16), piece)
        zsend[d] = zsum[at, :].astype(BF16)
        zc[d] = rcopy(zsend.at[d], zrecv.at[d], zs.at[d], zr.at[d], zdev[d])
        zc[d].start()
    total = zsum[pl.ds(pl.multiple_of(z * piece, 16), piece), :]
    for d in (1, 7, 2, 6, 3, 5, 4):
        zc[d].wait_recv()
        total = total + zrecv[d].astype(F32)
    tsend[...] = jnp.zeros_like(tsend)
    for i in range(2 * NY):
        tsend[i, 0:5, :] = total[5 * i : 5 * i + 5, :]
    tc = {}
    for d in range(1, 2 * NY):
        tc[d] = rcopy(
            tsend.at[lax.rem(ctx + d, 2 * NY)], trecv.at[d], ts.at[d], tr.at[d], tdev[d]
        )
        tc[d].start()
    same_core = tsend[ctx]
    other_core = jnp.zeros((8, N), F32)
    for d in range(1, 2 * NY):
        tc[d].wait_recv()
        if d % 2 == 0:
            same_core = same_core + trecv[d]
        else:
            other_core = other_core + trecv[d]
    grad_ref[:, :N] = jnp.where(first, same_core, other_core)[:5]
    grad_ref[:, N:] = jnp.where(first, other_core, same_core)[:5]
    for group in (copies, relays, pc, xc, zc, tc):
        for one in group.values():
            one.wait_send()
    own_relay.wait_send()
    for one in swap:
        one.wait_send()


VMEM = pl.BlockSpec(memory_space=pltpu.VMEM)
DMA = pltpu.SemaphoreType.DMA


def body(u_codes, u_scale, w_bc, xs, dt, log_keep, dy, lengths):
    v = pltpu.VMEM
    offset = lax.axis_index("ctx") * CH
    at = lengths[0, 0] - offset
    r_eff = jnp.where(at < 0, 1 << 20, at)
    r_end = jnp.where(r_eff < CH, r_eff, 0)
    limit = jnp.where(offset > 0, r_eff, 0)
    marks = jnp.stack([r_eff, r_end, limit]).astype(jnp.int32)
    hp = H * P_SIZE
    span = D // NX
    grad, gdt, gkeep = pl.pallas_call(
        mixer_kernel,
        out_shape=(
            jax.ShapeDtypeStruct((5, 2 * N), F32),
            jax.ShapeDtypeStruct((H, CH), F32),
            jax.ShapeDtypeStruct((H, CH), F32),
        ),
        in_specs=[pl.BlockSpec(memory_space=pltpu.SMEM)] + [VMEM] * 7,
        out_specs=(VMEM,) * 3,
        scratch_shapes=[
            v((D, CH), BF16), v((D, 2 * N), BF16), v((CH, D), BF16),
            v((2, CH, hp), BF16), v((2, CH, hp), BF16), v((hp, N), F32), v((hp, N), F32),
            v((HALF, N), F32), v((HALF, N), F32),
            v((H, 128), F32), v((H, 128), F32),
            v((HALF, N), BF16), v((HALF, N), BF16), v((HALF, N), BF16), v((HALF, N), BF16),
            v((hp, N), F32), v((hp, N), F32), v((HALF, N), F32), v((HALF, N), F32),
            v((CH, 128), F32), v((H, CH), F32), v((CH, CH), F32), v((CH, CH), F32), v((CH, CH), F32),
            v((H, CH), F32), v((CH, 128), F32), v((CH, 128), F32), v((CH, 128), F32), v((CH, 128), F32),
            v((NX, span, N), F32), v((NX, span, N), F32), v((NX, span, N), F32),
            v((6, span // 2, N), BF16), v((6, span // 2, N), BF16), v((span, N), F32),
            v((NZ, span // NZ, N), BF16), v((NZ, span // NZ, N), BF16),
            v((2 * NY, 8, N), F32), v((2 * NY, 8, N), F32),
            DMA((16,)), DMA((16,)), DMA((17,)), DMA((17,)), DMA,
            DMA((3,)), DMA((3,)),
        ] + [DMA((NCHUNK,))] * 8 + [
            DMA((NX,)), DMA((NX,)), DMA((6,)), DMA((6,)), DMA((NZ,)), DMA((NZ,)),
            DMA((2 * NY,)), DMA((2 * NY,)),
        ],
        compiler_params=pltpu.CompilerParams(
            collective_id=0, has_side_effects=True, vmem_limit_bytes=60 * 1024 * 1024
        ),
        name="mixer",
    )(marks, u_codes[0], u_scale[0].T, w_bc, xs[0], dy[0], dt[0], log_keep[0])
    return grad, gdt[None], gkeep[None]


def solution(mesh):
    placed = (
        P("dp", "ctx", None),
        P("dp", "ctx", None),
        P("ctx", None),
        P("dp", "ctx", None),
        P("dp", None, "ctx"),
        P("dp", None, "ctx"),
        P("dp", "ctx", None),
        P("dp", None),
    )
    return jax.shard_map(
        body,
        mesh=mesh,
        in_specs=placed,
        out_specs=(P(("dp", "ctx"), None), P("dp", None, "ctx"), P("dp", None, "ctx")),
        check_vma=False,
    )
```
